512 devices in a mesh: seq: 64 (over z, x, core), head: 8 (over y).
Axes of the slice: x: 4, y: 8, z: 8, core: 2. Of those that a mesh axis runs over, the one named last changes fastest.
Arguments:
- query_states: bfloat16 [16384, 4096], P(('seq', 'head')), may hold values from -8 to 8
- key_states: bfloat16 [16384, 4096], P(('seq', 'head')), may hold values from -8 to 8
- value_states: bfloat16 [16384, 4096], P(('seq', 'head')), may hold values from -8 to 8
- out_grad: bfloat16 [16384, 4096], P(('seq', 'head')), may hold values from -6 to 6
Outputs:
- attended: bfloat16 [16384, 4096], P('seq', 'head')
- query_grad: bfloat16 [16384, 4096], P('seq', 'head')
- key_grad: bfloat16 [16384, 4096], P('seq', 'head')
- value_grad: bfloat16 [16384, 4096], P('seq', 'head')
The draws below stay inside these ranges and needn't reach their ends.
All inputs are finite; a program needn't handle non-finite values.
Results may differ from the reference program's by a relative error of at most 0.025.
Values may be sent and summed in bfloat16 or wider, within the bound.
A program may use at most 64 MiB of HBM per device.

```python
import jax
import jax.numpy as jnp
from jax import lax

HEADS = 32
HEAD_DIM = 128
BLOCK = 128
TOK_DEV = 256
WIDTH = 4096
TOKENS = 16384


def shared_lift(key):
    base = jax.random.fold_in(key, 7003)
    coins = jax.random.bernoulli(base, 0.5, (1, WIDTH))
    direction = jnp.where(coins, 1.0, -1.0).astype(jnp.float32)
    strength = (jnp.log(jnp.float32(TOKENS / TOK_DEV)) / HEAD_DIM ** 0.5) ** 0.5
    return strength * direction


def region_offset(key, salt, spread, limit):
    regions = TOKENS // (2 * BLOCK)
    offset = spread * jax.random.truncated_normal(jax.random.fold_in(key, salt), -limit, limit, (regions, WIDTH), jnp.float32)
    return jnp.repeat(offset, 2 * BLOCK, axis=0)


def draw_query_states(key, part):
    lift = shared_lift(key)
    rows = jnp.arange(TOKENS)[:, None]
    drawn = jax.random.truncated_normal(jax.random.fold_in(key, 11), -4.0, 4.0, (TOKENS, WIDTH), jnp.float32)
    drawn = drawn + jnp.where(rows < BLOCK, lift, 0.0)
    return drawn.astype(jnp.bfloat16)


def draw_key_states(key, part):
    offset = region_offset(key, 12, 1.5, 2.0)
    lift = shared_lift(key)
    rows = jnp.arange(TOKENS)[:, None]
    lifted = jnp.where((rows >= TOK_DEV) & (rows < 2 * TOK_DEV), lift, 0.0)
    drawn = jax.random.truncated_normal(jax.random.fold_in(key, 13), -4.0, 4.0, (TOKENS, WIDTH), jnp.float32) + offset + lifted
    return drawn.astype(jnp.bfloat16)


def draw_value_states(key, part):
    offset = region_offset(key, 14, 1.0, 3.0)
    drawn = jax.random.truncated_normal(jax.random.fold_in(key, 15), -4.0, 4.0, (TOKENS, WIDTH), jnp.float32)
    return (drawn + offset).astype(jnp.bfloat16)


def levels(own_key, shape, cuts, low, high):
    factor_of = 1.0
    for axis_at, parts in cuts:
        heights = jax.random.uniform(jax.random.fold_in(jax.random.fold_in(own_key, 6), axis_at), (parts,), jnp.float32, low / len(cuts), high / len(cuts))
        factor_of = factor_of * jnp.repeat(jnp.exp(heights), shape[axis_at] // parts).reshape((-1,) + (1,) * (len(shape) - 1 - axis_at))
    return factor_of


def bell_draw(rng, shape, scale, bound, split=(), held_as=jnp.bfloat16):
    factor_of = levels(rng, shape, split, -0.22, 0.18) if split else 1.0
    entries = jax.random.normal(rng, shape, jnp.float32) * scale * factor_of
    return jnp.minimum(jnp.maximum(entries, -bound), bound).astype(held_as)


def setup_inputs(seed: int = 0) -> dict:
    key_list = jax.random.split(jax.random.key(seed), 5)
    return {
        "query_states": draw_query_states(jax.random.fold_in(key_list[4], 71), 0),
        "key_states": draw_key_states(jax.random.fold_in(key_list[4], 71), 0),
        "value_states": draw_value_states(jax.random.fold_in(key_list[4], 71), 0),
        "out_grad": bell_draw(key_list[3], (TOKENS, WIDTH), 1.0, 6.0, ((0, 512),)),
    }


MASKED = -1e30


def neighbours(blocked):
    zero_block = jnp.zeros((1,) + blocked.shape[1:], blocked.dtype)
    before = jnp.concatenate([zero_block, blocked[:-1]], 0)
    after = jnp.concatenate([blocked[1:], zero_block], 0)
    shared = jnp.broadcast_to(blocked[:1], blocked.shape)
    return jnp.concatenate([shared, before, blocked, after], 1)[1:]


def fold_back(grads, block_count):
    pieces = grads.reshape(block_count - 1, 4, BLOCK, HEAD_DIM)
    total = jnp.zeros((block_count, BLOCK, HEAD_DIM), jnp.float32)
    total = total.at[0].add(jnp.sum(pieces[:, 0], 0))
    total = total.at[:-1].add(pieces[:, 1])
    total = total.at[1:].add(pieces[:, 2])
    total = total.at[2:].add(pieces[:-1, 3])
    return total


def head_pass(arrays):
    query_rows, key_rows, value_rows, grad_rows = arrays
    inverse_square_root = HEAD_DIM ** -0.5
    block_count = TOKENS // BLOCK
    query_blocks = query_rows.reshape(block_count, BLOCK, HEAD_DIM)
    key_blocks = key_rows.reshape(block_count, BLOCK, HEAD_DIM)
    value_blocks = value_rows.reshape(block_count, BLOCK, HEAD_DIM)
    grad_blocks = grad_rows.reshape(block_count, BLOCK, HEAD_DIM)
    window_key_rows = neighbours(key_blocks)
    window_value_rows = neighbours(value_blocks)
    following_queries = query_blocks[1:]
    following_gradients = grad_blocks[1:]
    block_ids = jnp.arange(1, block_count)
    allowed = jnp.stack([block_ids >= 2, block_ids >= 1, block_ids >= 0, block_ids + 1 < block_count], 1)
    allowed = jnp.repeat(allowed, BLOCK, axis=1)[:, None, :]
    logit_scores = jnp.einsum("igc,imc->igm", following_queries.astype(jnp.float32), window_key_rows.astype(jnp.float32)) * inverse_square_root
    logit_scores = jnp.where(allowed, logit_scores, MASKED)
    row_top = jnp.max(logit_scores, -1, keepdims=True)
    log_total = row_top + jnp.log(jnp.sum(jnp.exp(logit_scores - row_top), -1, keepdims=True))
    weights = jnp.where(allowed, jnp.exp(logit_scores - log_total), 0.0)
    probabilities = weights.astype(jnp.bfloat16)
    window_output = jnp.einsum("hli,hix->hlx", probabilities.astype(jnp.float32), window_value_rows.astype(jnp.float32)).astype(jnp.bfloat16)
    glob_scores = jnp.dot(query_blocks[0], key_rows.T, preferred_element_type=jnp.float32) * inverse_square_root
    glob_top = jnp.max(glob_scores, -1, keepdims=True)
    glob_log = glob_top + jnp.log(jnp.sum(jnp.exp(glob_scores - glob_top), -1, keepdims=True))
    glob_weights = jnp.exp(glob_scores - glob_log)
    glob_probs = glob_weights.astype(jnp.bfloat16)
    glob_out = jnp.dot(glob_probs, value_rows, preferred_element_type=jnp.float32).astype(jnp.bfloat16)
    attended = jnp.concatenate([glob_out[None], window_output], 0).reshape(TOKENS, HEAD_DIM)
    band_delta = jnp.sum(following_gradients.astype(jnp.float32) * window_output.astype(jnp.float32), -1, keepdims=True)
    probability_gradient = jnp.einsum("igc,imc->igm", following_gradients.astype(jnp.float32), window_value_rows.astype(jnp.float32))
    score_gradient = (weights * (probability_gradient - band_delta)).astype(jnp.bfloat16)
    window_query_gradient = jnp.einsum("hli,hix->hlx", score_gradient.astype(jnp.float32), window_key_rows.astype(jnp.float32)) * inverse_square_root
    window_key_gradient = jnp.einsum("lpe,lpo->leo", score_gradient.astype(jnp.float32), following_queries.astype(jnp.float32)) * inverse_square_root
    window_value_gradient = jnp.einsum("lpe,lpo->leo", probabilities.astype(jnp.float32), following_gradients.astype(jnp.float32))
    glob_delta = jnp.sum(grad_blocks[0].astype(jnp.float32) * glob_out.astype(jnp.float32), -1, keepdims=True)
    glob_dprob = jnp.dot(grad_blocks[0], value_rows.T, preferred_element_type=jnp.float32)
    glob_dscore = (glob_weights * (glob_dprob - glob_delta)).astype(jnp.bfloat16)
    glob_dquery = jnp.dot(glob_dscore, key_rows, preferred_element_type=jnp.float32) * inverse_square_root
    key_extra = jnp.dot(glob_dscore.T, query_blocks[0], preferred_element_type=jnp.float32) * inverse_square_root
    value_extra = jnp.dot(glob_probs.T, grad_blocks[0], preferred_element_type=jnp.float32)
    key_grad = fold_back(window_key_gradient, block_count).reshape(TOKENS, HEAD_DIM) + key_extra
    value_grad = fold_back(window_value_gradient, block_count).reshape(TOKENS, HEAD_DIM) + value_extra
    query_grad = jnp.concatenate([glob_dquery[None], window_query_gradient], 0).reshape(TOKENS, HEAD_DIM)
    return (attended, query_grad.astype(jnp.bfloat16), key_grad.astype(jnp.bfloat16), value_grad.astype(jnp.bfloat16))


def reference(query_states, key_states, value_states, out_grad):
    def by_head(array):
        return array.reshape(TOKENS, HEADS, HEAD_DIM).transpose(1, 0, 2)

    def by_token(array):
        return array.transpose(1, 0, 2).reshape(TOKENS, HEADS * HEAD_DIM)

    results = lax.map(head_pass, (by_head(query_states), by_head(key_states), by_head(value_states), by_head(out_grad)))
    return (by_token(results[0]), by_token(results[1]), by_token(results[2]), by_token(results[3]))
```

```python
import jax
import jax.numpy as jnp
import numpy as np
from jax import lax
from jax.sharding import Mesh
from jax.sharding import PartitionSpec as P

HEAD_DIM = 128
BLOCK = 128


def seq_parts(mesh):
    column = mesh.devices[:, 0]
    count = column.shape[0]
    try:
        cores = len({d.core_on_chip for d in column})
        xs = len({d.coords[0] for d in column})
    except AttributeError:
        return (("s0", count),)
    parts = [("sz", count // (xs * cores)), ("sx", xs), ("sc", cores)]
    if parts[0][1] * xs * cores != count:
        return (("s0", count),)
    return tuple(p for p in parts if p[1] > 1) or (("s0", count),)


def make_local(parts):
    seq = tuple(name for name, _ in parts)
    seq_count = int(np.prod([size for _, size in parts]))

    def hpsum(value):
        for name in reversed(seq):
            value = lax.psum(value, name)
        return value

    def hgather(value):
        for name in reversed(seq):
            value = lax.all_gather(value, name, axis=0, tiled=True)
        return value

    def shifted(value, steps):
        leading, last = (max(0, -steps), min(seq_count, seq_count - steps))
        return lax.ppermute(value, seq, [(s, s + steps) for s in range(leading, last)])

    def local(query_states, key_states, value_states, out_grad):
        stacked = jnp.stack([query_states, key_states, value_states, out_grad])
        stacked = lax.all_to_all(stacked, "head", split_axis=2, concat_axis=1, tiled=True)
        local_rows = stacked.shape[1]
        head_count = stacked.shape[2] // HEAD_DIM
        block_count = local_rows // BLOCK
        position = lax.axis_index(seq)
        total_blocks = block_count * seq_count
        inverse_square_root = HEAD_DIM ** (-0.5)
        query_states, key_states, value_states, out_grad = (
            stacked[0], stacked[1], stacked[2], stacked[3]
        )

        def as_blocks(array):
            return array.reshape(block_count, BLOCK, head_count, HEAD_DIM)

        def as_heads(array):
            return array.reshape(array.shape[0], head_count, HEAD_DIM)

        leading = stacked[:, :BLOCK]
        leading = jnp.where(position == 0, leading, jnp.zeros_like(leading))
        leading = hpsum(leading)
        glob_query = as_heads(leading[0])
        glob_key = as_heads(leading[1])
        glob_value = as_heads(leading[2])
        glob_grad = as_heads(leading[3])

        kv = stacked[1:3]
        from_before = shifted(kv[:, local_rows - BLOCK :], 1)
        from_after = shifted(kv[:, :BLOCK], -1)
        extended = jnp.concatenate([from_before, kv, from_after], axis=1)

        def windows(rows_ext, shared):
            spread = jnp.broadcast_to(shared[None], (block_count, BLOCK, head_count, HEAD_DIM))
            return jnp.concatenate(
                [
                    spread,
                    as_blocks(rows_ext[:local_rows]),
                    as_blocks(rows_ext[BLOCK : BLOCK + local_rows]),
                    as_blocks(rows_ext[2 * BLOCK :]),
                ],
                1,
            )

        window_key_rows = windows(extended[0], glob_key)
        window_value_rows = windows(extended[1], glob_value)
        block_ids = position * block_count + jnp.arange(block_count)
        allowed = jnp.stack(
            [block_ids >= 2, block_ids >= 1, block_ids >= 0, block_ids + 1 < total_blocks], 1
        )
        allowed = jnp.repeat(allowed, BLOCK, axis=1)[:, None, None, :]
        live_rows = (block_ids != 0)[:, None, None, None]
        query_blocks = as_blocks(query_states)
        grad_blocks = as_blocks(out_grad)
        logit_scores = (
            jnp.einsum(
                "cqhd,ckhd->chqk", query_blocks, window_key_rows, preferred_element_type=jnp.float32
            )
            * inverse_square_root
        )
        logit_scores = jnp.where(allowed, logit_scores, -1e30)
        row_top = jnp.max(logit_scores, -1, keepdims=True)
        log_total = row_top + jnp.log(jnp.sum(jnp.exp(logit_scores - row_top), -1, keepdims=True))
        weights = jnp.where(allowed & live_rows, jnp.exp(logit_scores - log_total), 0.0)
        probabilities = weights.astype(jnp.bfloat16)
        window_output = jnp.einsum(
            "chqk,ckhd->cqhd", probabilities, window_value_rows, preferred_element_type=jnp.float32
        ).astype(jnp.bfloat16)

        local_keys = as_heads(key_states)
        local_values = as_heads(value_states)
        glob_scores = (
            jnp.einsum("qhd,khd->hqk", glob_query, local_keys, preferred_element_type=jnp.float32)
            * inverse_square_root
        )
        local_top = jnp.max(glob_scores, -1)
        local_exp = jnp.exp(glob_scores - local_top[:, :, None])
        local_sum = jnp.sum(local_exp, -1)
        local_out = jnp.einsum(
            "hqk,khd->hqd", local_exp, local_values.astype(jnp.float32),
            preferred_element_type=jnp.float32,
        )
        local_delta = jnp.sum(
            local_out * glob_grad.astype(jnp.float32).transpose(1, 0, 2), -1
        )
        stats = hgather(jnp.stack([local_top, local_sum, local_delta])[None])
        glob_top = jnp.max(stats[:, 0], 0)
        rescale = jnp.exp(stats[:, 0] - glob_top[None])
        glob_total = jnp.sum(rescale * stats[:, 1], 0)
        glob_log = glob_top + jnp.log(glob_total)
        glob_delta = jnp.sum(rescale * stats[:, 2], 0) / glob_total
        glob_weights = jnp.exp(glob_scores - glob_log[:, :, None])
        glob_probs = glob_weights.astype(jnp.bfloat16)
        glob_part = jnp.einsum(
            "hqk,khd->qhd", glob_probs, local_values, preferred_element_type=jnp.float32
        )
        glob_dprob = jnp.einsum(
            "qhd,khd->hqk", glob_grad, local_values, preferred_element_type=jnp.float32
        )
        glob_dscore = (glob_weights * (glob_dprob - glob_delta[:, :, None])).astype(jnp.bfloat16)
        glob_dquery_part = (
            jnp.einsum("hqk,khd->qhd", glob_dscore, local_keys, preferred_element_type=jnp.float32)
            * inverse_square_root
        )
        key_from_glob = (
            jnp.einsum("hqk,qhd->khd", glob_dscore, glob_query, preferred_element_type=jnp.float32)
            * inverse_square_root
        )
        value_from_glob = jnp.einsum(
            "hqk,qhd->khd", glob_probs, glob_grad, preferred_element_type=jnp.float32
        )
        band_delta = jnp.sum(
            grad_blocks.astype(jnp.float32) * window_output.astype(jnp.float32), -1
        ).transpose(0, 2, 1)
        probability_gradient = jnp.einsum(
            "cqhd,ckhd->chqk", grad_blocks, window_value_rows, preferred_element_type=jnp.float32
        )
        score_gradient = (weights * (probability_gradient - band_delta[:, :, :, None])).astype(
            jnp.bfloat16
        )
        window_query_gradient = (
            jnp.einsum(
                "chqk,ckhd->cqhd", score_gradient, window_key_rows, preferred_element_type=jnp.float32
            )
            * inverse_square_root
        )
        window_key_gradient = (
            jnp.einsum(
                "chqk,cqhd->ckhd", score_gradient, query_blocks, preferred_element_type=jnp.float32
            )
            * inverse_square_root
        )
        window_value_gradient = jnp.einsum(
            "chqk,cqhd->ckhd", probabilities, grad_blocks, preferred_element_type=jnp.float32
        )
        stacked_grads = jnp.stack([window_key_gradient, window_value_gradient]).reshape(
            2, block_count, 4, BLOCK, head_count, HEAD_DIM
        )
        glob_piece = jnp.sum(stacked_grads[:, :, 0], 1)
        before = stacked_grads[:, :, 1]
        middle = stacked_grads[:, :, 2]
        after = stacked_grads[:, :, 3]
        empty_block = jnp.zeros((2, 1, BLOCK, head_count, HEAD_DIM), jnp.float32)
        inner = (
            middle
            + jnp.concatenate([before[:, 1:], empty_block], 1)
            + jnp.concatenate([empty_block, after[:, :-1]], 1)
        )
        from_right = shifted(before[:, 0].astype(jnp.bfloat16), -1).astype(jnp.float32)
        from_left = shifted(after[:, -1].astype(jnp.bfloat16), 1).astype(jnp.float32)
        inner = inner.at[:, 0].add(from_left)
        inner = inner.at[:, -1].add(from_right)
        glob_out, glob_dquery, glob_dkey, glob_dvalue = hpsum(
            (glob_part, glob_dquery_part, glob_piece[0], glob_piece[1])
        )
        glob_out = glob_out.astype(jnp.bfloat16)
        local_grads = inner.reshape(2, local_rows, head_count, HEAD_DIM) + jnp.stack(
            [key_from_glob, value_from_glob]
        )
        is_first = ((jnp.arange(local_rows) < BLOCK) & (position == 0))[:, None, None]

        def padded(array):
            return jnp.concatenate(
                [array, jnp.zeros((local_rows - BLOCK,) + array.shape[1:], array.dtype)], 0
            )

        key_grad = local_grads[0] + jnp.where(is_first, padded(glob_dkey), 0.0)
        value_grad = local_grads[1] + jnp.where(is_first, padded(glob_dvalue), 0.0)
        query_grad = jnp.where(
            is_first,
            padded(glob_dquery),
            window_query_gradient.reshape(local_rows, head_count, HEAD_DIM),
        )
        attended = jnp.where(
            is_first, padded(glob_out), window_output.reshape(local_rows, head_count, HEAD_DIM)
        )
        return (
            attended.reshape(local_rows, -1),
            query_grad.reshape(local_rows, -1).astype(jnp.bfloat16),
            key_grad.reshape(local_rows, -1).astype(jnp.bfloat16),
            value_grad.reshape(local_rows, -1).astype(jnp.bfloat16),
        )

    return local, seq


def solution(mesh):
    parts = seq_parts(mesh)
    heads = mesh.shape["head"]
    names = tuple(name for name, _ in parts)
    sizes = tuple(size for _, size in parts)
    split_mesh = Mesh(mesh.devices.reshape(sizes + (heads,)), names + ("head",))
    local, seq = make_local(parts)
    spec_in = P(seq + ("head",), None)
    spec_out = P(seq, "head")
    return jax.shard_map(
        local,
        mesh=split_mesh,
        in_specs=(spec_in,) * 4,
        out_specs=(spec_out,) * 4,
        check_vma=False,
    )
```
